32 devices in a mesh: parts: 2 (over y), row: 4 (over z), frame: 4 (over x, core).
Axes of the slice: x: 2, y: 2, z: 4, core: 2. Of those that a mesh axis runs over, the one named last changes fastest.
Arguments:
- latent: bfloat16 [8, 8, 16, 512], P(('parts', 'frame'), 'row'), parts along dimension 0, may hold values from -15 to 15
- qkv_weight: bfloat16 [3, 512, 512], P(None, 'frame'), may hold values from -0.125 to 0.125
- out_weight: bfloat16 [512, 512], P('frame'), may hold values from -0.25 to 0.25
- attn_gain: float32 [512], replicated, may hold values from 0.1 to 1.9
- in_weight: bfloat16 [512, 2, 2048], P(None, None, 'frame'), may hold values from -0.25 to 0.25
- depth_weight: float32 [3, 3, 2, 2048], replicated, may hold values from -2 to 2
- down_weight: bfloat16 [2048, 512], P('frame'), may hold values from -0.125 to 0.125
- mlp_gain: float32 [512], replicated, may hold values from 0.1 to 1.9
- conv_first: bfloat16 [3, 3, 3, 512, 512], P(None, None, None, 'frame'), may hold values from -0.0546875 to 0.0546875
- conv_second: bfloat16 [3, 3, 3, 512, 512], P(None, None, None, 'frame'), may hold values from -0.0546875 to 0.0546875
Outputs:
- decoded: bfloat16 [8, 8, 16, 512], P('parts', 'row', 'frame'), parts along dimension 0
The draws below stay inside these ranges and needn't reach their ends.
There are 2 independent parts, one for each index of `parts`. The reference program is written for one: setup_inputs(seed, part) draws one part's arguments, and reference() takes and returns one part's arrays. A program takes and returns all parts, laid end to end along the dimension named above; an argument that names none is the same for every part. Nothing has to cross between parts.
All inputs are finite; a program needn't handle non-finite values.
Results may differ from the reference program's by a relative error of at most 0.015.
Values may be sent and summed in bfloat16 or wider, within the bound.
A program may use at most 128 MiB of HBM per device.

```python
import jax
import jax.numpy as jnp
from jax import lax

CH = 512
HEAD = 32
INNER = 2048
COLS = 16
FRAMES = 4
HEIGHT = 8


def draw_latent(key, part):
    shape = (FRAMES, HEIGHT, COLS, CH)
    ramp = 1.0 + 2.0 * jnp.arange(HEIGHT, dtype=jnp.float32) / max(HEIGHT - 1, 1)
    values = jax.random.normal(jax.random.fold_in(key, 7), shape, jnp.float32) * ramp[None, :, None, None]
    return jnp.clip(values, -15.0, 15.0).astype(jnp.bfloat16)


def level_of(stream_key, dims, shards, low, largest):
    factor_of = 1.0
    for axis_at, shards_of in shards:
        draws = jax.random.uniform(jax.random.fold_in(jax.random.fold_in(stream_key, 6), axis_at), (shards_of,), jnp.float32, low / len(shards), largest / len(shards))
        factor_of = factor_of * jnp.repeat(jnp.exp(draws), dims[axis_at] // shards_of).reshape((-1,) + (1,) * (len(dims) - 1 - axis_at))
    return factor_of


def gaussian(own_key, extent, scale, limit, pieces=(), kind=jnp.bfloat16):
    level = level_of(own_key, extent, pieces, -0.22, 0.18) if pieces else 1.0
    result = jax.random.normal(own_key, extent, jnp.float32) * scale * level
    return jnp.minimum(jnp.maximum(result, -limit), limit).astype(kind)


def setup_inputs(seed: int = 0, part: int = 0) -> dict:
    splits = jax.random.split(jax.random.key(seed), 11)
    part_splits = jax.random.split(jax.random.fold_in(splits[10], part), 11)
    return {
        "latent": draw_latent(jax.random.fold_in(jax.random.fold_in(splits[10], part), 71), part),
        "qkv_weight": gaussian(splits[1], (3, CH, CH), (4 * CH) ** -0.5, 0.125, ((1, 4),)),
        "out_weight": gaussian(splits[2], (CH, CH), CH ** -0.5, 0.25, ((0, 4),)),
        "attn_gain": jnp.clip(1.0 + 0.18 * jax.random.normal(splits[3], (CH,), jnp.float32), 0.1, 1.9),
        "in_weight": gaussian(splits[4], (CH, 2, INNER), CH ** -0.5, 0.25, ((2, 4),)),
        "depth_weight": gaussian(splits[5], (3, 3, 2, INNER), 9 ** -0.5, 2.0, (), jnp.float32),
        "down_weight": gaussian(splits[6], (INNER, CH), INNER ** -0.5, 0.125, ((0, 4),)),
        "mlp_gain": jnp.clip(1.0 + 0.18 * jax.random.normal(splits[7], (CH,), jnp.float32), 0.1, 1.9),
        "conv_first": gaussian(splits[8], (3, 3, 3, CH, CH), (27 * CH) ** -0.5, 0.0546875, ((3, 4),)),
        "conv_second": gaussian(splits[9], (3, 3, 3, CH, CH), (27 * CH) ** -0.5, 0.0546875, ((3, 4),)),
    }


def norm_rows(values, gain):
    return values * lax.rsqrt(lax.optimization_barrier(jnp.mean(values * values, axis=-1, keepdims=True)) + 1e-05) * gain

def conv_full(field, kernel):
    kernel_io = jnp.transpose(kernel, (0, 1, 2, 4, 3))
    return lax.conv_general_dilated(field[None].astype(jnp.float32), kernel_io.astype(jnp.float32), (1, 1, 1), ((1, 1), (1, 1), (1, 1)), dimension_numbers=('NDHWC', 'DHWIO', 'NDHWC'), precision=lax.Precision.HIGHEST)[0]

def reference(latent, qkv_weight, out_weight, attn_gain, in_weight, depth_weight, down_weight, mlp_gain, conv_first, conv_second):
    frames, height, columns, width = latent.shape
    heads = width // HEAD
    flat_in = latent.reshape(-1, width)
    packed = jnp.dot(flat_in, qkv_weight.reshape(3 * width, width).T, preferred_element_type=jnp.float32).astype(jnp.bfloat16)
    packed = packed.reshape(frames, height * columns, 3, heads, HEAD)
    query = jnp.maximum(packed[:, :, 0], 0).astype(jnp.float32)
    keys = jnp.maximum(packed[:, :, 1], 0).astype(jnp.float32)
    values = packed[:, :, 2].astype(jnp.float32)
    count = height * columns
    state = jnp.einsum('fnhd,fnhe->fhde', keys, values, precision=lax.Precision.HIGHEST) / count
    key_mean = lax.optimization_barrier(jnp.sum(keys, axis=1)) / count
    numer = jnp.einsum('fnhd,fhde->fnhe', query, state, precision=lax.Precision.HIGHEST)
    denom = jnp.maximum(jnp.einsum('fnhd,fhd->fnh', query, key_mean, precision=lax.Precision.HIGHEST), 1.0)
    mixed = (numer / denom[..., None]).astype(jnp.bfloat16).reshape(-1, width)
    attn_out = jnp.dot(mixed, out_weight, preferred_element_type=jnp.float32)
    first = (flat_in.astype(jnp.float32) + norm_rows(attn_out, attn_gain)).astype(jnp.bfloat16)
    inner = jax.nn.silu(jnp.dot(first, in_weight.reshape(width, -1), preferred_element_type=jnp.float32)).astype(jnp.bfloat16)
    inner = inner.reshape(frames, height, columns, 2, -1)
    padded = jnp.pad(inner, ((0, 0), (1, 1), (1, 1), (0, 0), (0, 0)))
    spread = jnp.zeros(inner.shape, jnp.float32)
    for shift_row in range(3):
        for shift_col in range(3):
            spread = spread + padded[:, shift_row:shift_row + height, shift_col:shift_col + columns].astype(jnp.float32) * depth_weight[shift_row, shift_col]
    gated = (spread[..., 0, :] * jax.nn.silu(spread[..., 1, :])).astype(jnp.bfloat16)
    mlp_out = jnp.dot(gated.reshape(frames * height * columns, -1), down_weight, preferred_element_type=jnp.float32)
    second = (first.astype(jnp.float32) + norm_rows(mlp_out, mlp_gain)).astype(jnp.bfloat16)
    second = second.reshape(frames, height, columns, width)
    hidden_conv = jax.nn.silu(conv_full(second, conv_first)).astype(jnp.bfloat16)
    return (second.astype(jnp.float32) + conv_full(hidden_conv, conv_second)).astype(jnp.bfloat16)
```

```python
import functools

import jax
import jax.numpy as jnp
from jax import lax
from jax.experimental import pallas as pl
from jax.experimental.pallas import tpu as pltpu
from jax.sharding import PartitionSpec as P

HEAD = 32
F32 = jnp.float32
BF16 = jnp.bfloat16
MESH = pl.DeviceIdType.MESH


def dot(a, b):
    return jnp.dot(a, b, preferred_element_type=F32)


def dot_nt(a, b):
    return lax.dot_general(a, b, (((1,), (1,)), ((), ())), preferred_element_type=F32)


def dot_tn(a, b):
    return lax.dot_general(a, b, (((0,), (0,)), ((), ())), preferred_element_type=F32)


def split(values):
    high = values.astype(BF16)
    return high, (values - high.astype(F32)).astype(BF16)


def norm_rows(values, gain):
    return values * lax.rsqrt(jnp.mean(values * values, axis=-1, keepdims=True) + 1e-05) * gain


def column_shifts(flat, columns):
    count = flat.shape[0]
    at = lax.rem(lax.broadcasted_iota(jnp.int32, flat.shape, 0), columns)
    left = jnp.where(at == 0, 0.0, pltpu.roll(flat, 1, 0))
    right = jnp.where(at == columns - 1, 0.0, pltpu.roll(flat, count - 1, 0))
    return left, flat, right


def kernel(
    F,
    R,
    latent_ref,
    qkv_ref,
    out_w_ref,
    attn_gain_ref,
    in_w_hbm,
    depth_ref,
    down_hbm,
    mlp_gain_ref,
    first_hbm,
    second_hbm,
    out_ref,
    x_buf,
    ow_buf,
    st_buf,
    mx_buf,
    fi_buf,
    part_buf,
    rs_send,
    rs_buf,
    own_buf,
    s_buf,
    sh_buf,
    h_buf,
    hs_buf,
    fs_buf,
    fr_buf,
    in_w,
    down_w,
    first_w,
    second_w,
    load_sem,
    x_ssem,
    x_rsem,
    ow_ssem,
    ow_rsem,
    st_ssem,
    st_rsem,
    mx_ssem,
    mx_rsem,
    rs_ssem,
    rs_rsem,
    s_ssem,
    s_rsem,
    h_ssem,
    h_rsem,
    f_ssem,
    f_rsem,
):
    me_f = lax.axis_index("frame")
    me_r = lax.axis_index("row")
    fl, h, W, C = latent_ref.shape
    T = fl * F
    hc = qkv_ref.shape[1]
    N = in_w.shape[2]
    oc = first_w.shape[3]
    heads = hc // HEAD
    wc = W // F

    loads = [
        pltpu.make_async_copy(src, dst, load_sem.at[i])
        for i, (src, dst) in enumerate(
            ((in_w_hbm, in_w), (down_hbm, down_w), (first_hbm, first_w), (second_hbm, second_w))
        )
    ]
    for load in loads:
        load.start()

    def ahead(d):
        return lax.rem(me_f + d, F)

    def behind(d):
        return lax.rem(me_f + (F - d), F)

    def remote(src, dst, ssem, rsem, row, frame):
        return pltpu.make_async_remote_copy(
            src_ref=src,
            dst_ref=dst,
            send_sem=ssem,
            recv_sem=rsem,
            device_id={"row": row, "frame": frame},
            device_id_type=MESH,
        )

    barrier = pltpu.get_barrier_semaphore()

    def greet(row, frame):
        pl.semaphore_signal(barrier, inc=1, device_id={"row": row, "frame": frame}, device_id_type=MESH)

    for d in range(1, F):
        greet(me_r, ahead(d))
    for d in range(1, R):
        greet(lax.rem(me_r + d, R), me_f)

    @pl.when(me_r < R - 1)
    def _():
        for d in range(1, F):
            greet(me_r + 1, ahead(d))

    @pl.when(me_r > 0)
    def _():
        for d in range(1, F):
            greet(me_r - 1, ahead(d))

    neighbours = lax.div(me_r + (R - 1), R) + lax.div(2 * R - 2 - me_r, R)
    pl.semaphore_wait(barrier, F - 1 + R - 1 + (F - 1) * neighbours)

    def frames_of(index):
        return pl.ds(index * fl, fl)

    def band_start(src, buf, g, ssem, rsem):
        mine = frames_of(me_f)

        @pl.when(me_r < R - 1)
        def _():
            for d in range(F):
                remote(
                    src.at[:, h - g : h], buf.at[mine, 0:g], ssem.at[F + d], rsem.at[F + d], me_r + 1, ahead(d)
                ).start()

        @pl.when(me_r > 0)
        def _():
            for d in range(F):
                remote(
                    src.at[:, 0:g], buf.at[mine, g + h : h + 2 * g], ssem.at[2 * F + d], rsem.at[2 * F + d],
                    me_r - 1, ahead(d),
                ).start()

        for d in range(1, F):
            remote(src, buf.at[mine, g : g + h], ssem.at[d], rsem.at[d], me_r, ahead(d)).start()

    def band_wait(src, buf, g, ssem, rsem):
        for d in range(1, F):
            remote(src, buf.at[frames_of(behind(d)), g : g + h], ssem.at[d], rsem.at[d], me_r, ahead(d)).wait()

        @pl.when(me_r > 0)
        def _():
            for d in range(F):
                theirs = frames_of(behind(d))
                remote(
                    src.at[:, 0:g], buf.at[theirs, 0:g], ssem.at[2 * F + d], rsem.at[F + d], me_r - 1, ahead(d)
                ).wait()

        @pl.when(me_r < R - 1)
        def _():
            for d in range(F):
                theirs = frames_of(behind(d))
                remote(
                    src.at[:, h - g : h], buf.at[theirs, g + h : h + 2 * g], ssem.at[F + d], rsem.at[2 * F + d],
                    me_r + 1, ahead(d),
                ).wait()

    def zero_edges(buf, g):
        @pl.when(me_r == 0)
        def _():
            buf[:, 0:g] = jnp.zeros((T, g, W, C), BF16)

        @pl.when(me_r == R - 1)
        def _():
            buf[:, g + h : h + 2 * g] = jnp.zeros((T, g, W, C), BF16)

    def share_start(buf, ssem, rsem, src=None):
        for d in range(1, F):
            remote(
                buf.at[me_f] if src is None else src, buf.at[me_f], ssem.at[d], rsem.at[d], me_r, ahead(d)
            ).start()

    def share_wait(buf, ssem, rsem, src=None):
        for d in range(1, F):
            remote(
                buf.at[me_f] if src is None else src, buf.at[behind(d)], ssem.at[d], rsem.at[d], me_r, ahead(d)
            ).wait()

    band_start(latent_ref, x_buf, 1, x_ssem, x_rsem)
    x_buf[frames_of(me_f), 1 : 1 + h] = latent_ref[...]
    zero_edges(x_buf, 1)
    zero_edges(s_buf, 2)
    ow_buf[me_f] = out_w_ref[...]
    for shift in range(3):
        for t in (0, T + 1):
            sh_buf[shift, t] = jnp.zeros(sh_buf.shape[2:], BF16)
            hs_buf[shift, t] = jnp.zeros(hs_buf.shape[2:], BF16)
    band_wait(latent_ref, x_buf, 1, x_ssem, x_rsem)
    share_start(ow_buf, ow_ssem, ow_rsem, out_w_ref)

    own_x = x_buf[:, 1 : 1 + h].reshape(T * h * W, C)
    keys = jnp.maximum(dot_nt(own_x, qkv_ref[1]), 0.0).astype(BF16)
    values = dot_nt(own_x, qkv_ref[2]).astype(BF16)
    head_row = lax.div(lax.broadcasted_iota(jnp.int32, (hc, hc), 0), HEAD)
    head_col = lax.div(lax.broadcasted_iota(jnp.int32, (hc, hc), 1), HEAD)
    same_head = head_row == head_col
    n = h * W
    for t in range(T):
        outer = dot_tn(keys[t * n : (t + 1) * n], values[t * n : (t + 1) * n])
        outer = jnp.where(same_head, outer, 0.0)
        packed = outer[0:HEAD]
        for i in range(1, heads):
            packed = packed + outer[i * HEAD : (i + 1) * HEAD]
        st_buf[me_r, t * HEAD : (t + 1) * HEAD] = packed.astype(BF16)
    sums = st_buf.shape[1] - T * HEAD
    of_frame = lax.div(lax.broadcasted_iota(jnp.int32, (sums, T * n), 1), n)
    pick = jnp.where(of_frame == lax.broadcasted_iota(jnp.int32, (sums, T * n), 0), 1.0, 0.0).astype(BF16)
    st_buf[me_r, T * HEAD :] = dot(pick, keys).astype(BF16)
    for d in range(1, R):
        remote(
            st_buf.at[me_r], st_buf.at[me_r], st_ssem.at[d], st_rsem.at[d], lax.rem(me_r + d, R), me_f
        ).start()
    query = jnp.maximum(dot_nt(x_buf[...].reshape(T * (h + 2) * W, C), qkv_ref[0]), 0.0).astype(BF16)
    for d in range(1, R):
        remote(
            st_buf.at[me_r], st_buf.at[lax.rem(me_r + (R - d), R)], st_ssem.at[d], st_rsem.at[d],
            lax.rem(me_r + d, R), me_f,
        ).wait()
    total = st_buf[0].astype(F32)
    for r in range(1, R):
        total = total + st_buf[r].astype(F32)
    total = total * (1.0 / (h * R * W))

    ones = jnp.where(same_head, 1.0, 0.0).astype(BF16)
    m = (h + 2) * W
    for t in range(T):
        q = query[t * m : (t + 1) * m]
        packed = total[t * HEAD : (t + 1) * HEAD]
        state = jnp.where(same_head, jnp.concatenate([packed] * heads, axis=0), 0.0)
        high, low = split(state)
        numer = dot(q, high) + dot(q, low)
        high, low = split(q.astype(F32) * total[T * HEAD + t : T * HEAD + t + 1])
        denom = jnp.maximum(dot(high, ones) + dot(low, ones), 1.0)
        mx_buf[me_f, t * m : (t + 1) * m] = (numer / denom).astype(BF16)
    share_start(mx_buf, mx_ssem, mx_rsem)
    share_wait(ow_buf, ow_ssem, ow_rsem, out_w_ref)
    share_wait(mx_buf, mx_ssem, mx_rsem)

    attn_out = dot(mx_buf[0], ow_buf[0])
    for f in range(1, F):
        attn_out = attn_out + dot(mx_buf[f], ow_buf[f])
    latent = x_buf[...].reshape(T * m, C).astype(F32)
    first = (latent + norm_rows(attn_out, attn_gain_ref[...])).astype(BF16)
    fi_buf[...] = first.reshape(T, h + 2, W, C)

    loads[0].wait()
    spread = []
    lanes = pl.ds(pl.multiple_of(me_f * N, N), N)
    for k in range(2):
        inner = jax.nn.silu(dot(first, in_w[k])).astype(BF16).astype(F32)
        mix = jnp.zeros((T, h, W, N), F32)
        for j, moved in enumerate(column_shifts(inner, W)):
            moved = moved.reshape(T, h + 2, W, N)
            for i in range(3):
                tap = depth_ref[i, j, k : k + 1, lanes]
                mix = mix + moved[:, i : i + h] * tap.reshape(1, 1, 1, N)
        spread.append(mix)
    gated = (spread[0] * jax.nn.silu(spread[1])).astype(BF16).reshape(T * n, N)
    loads[1].wait()
    part = dot(gated, down_w[...]).reshape(T, h, W, C)
    part_buf[...] = part
    rs_send[...] = part.astype(BF16)
    for d in range(1, F):
        remote(
            rs_send.at[frames_of(ahead(d))], rs_buf.at[d], rs_ssem.at[d], rs_rsem.at[d], me_r, ahead(d)
        ).start()
    for d in range(1, F):
        remote(
            rs_send.at[frames_of(ahead(d))], rs_buf.at[d], rs_ssem.at[d], rs_rsem.at[d], me_r, ahead(d)
        ).wait()
    mlp_out = part_buf[frames_of(me_f)]
    for d in range(1, F):
        mlp_out = mlp_out + rs_buf[d].astype(F32)
    second = (
        fi_buf[frames_of(me_f), 1 : 1 + h].astype(F32)
        + norm_rows(mlp_out, mlp_gain_ref[...].reshape(1, 1, 1, C))
    ).astype(BF16)
    own_buf[...] = second
    band_start(own_buf, s_buf, 2, s_ssem, s_rsem)
    s_buf[frames_of(me_f), 2 : 2 + h] = second
    band_wait(own_buf, s_buf, 2, s_ssem, s_rsem)

    rows = h + 4
    for j, moved in enumerate(column_shifts(s_buf[...].reshape(T * rows * W, C).astype(F32), W)):
        sh_buf[j, 1 : T + 1] = moved.astype(BF16).reshape(T, rows, W, C)
    loads[2].wait()

    def conv(buf, weights, out_rows):
        acc = jnp.zeros((T * out_rows * W, oc), F32)
        for a in range(3):
            for b in range(3):
                for c in range(3):
                    slab = buf[c, a : a + T, b : b + out_rows].reshape(T * out_rows * W, C)
                    acc = acc + dot_nt(slab, weights[a, b, c])
        return acc

    active = jax.nn.silu(conv(sh_buf, first_w, h + 2))
    row = lax.rem(lax.div(lax.broadcasted_iota(jnp.int32, active.shape, 0), W), h + 2) + (me_r * h - 1)
    hidden = jnp.where((row >= 0) & (row < h * R), active, 0.0)
    h_buf[me_f] = hidden.astype(BF16)
    share_start(h_buf, h_ssem, h_rsem)
    loads[3].wait()
    share_wait(h_buf, h_ssem, h_rsem)
    for f in range(F):
        for j, moved in enumerate(column_shifts(h_buf[f].astype(F32), W)):
            hs_buf[j, 1 : T + 1, :, :, f * oc : (f + 1) * oc] = moved.astype(BF16).reshape(T, h + 2, W, oc)
    result = conv(hs_buf, second_w, h)
    for f in range(F):
        kept = s_buf[:, 2 : 2 + h, :, f * oc : (f + 1) * oc].astype(F32).reshape(T * n, oc)
        result = result + jnp.where(me_f == f, kept, 0.0)
    result = result.reshape(T, h, W, oc)
    for j in range(F):
        fs_buf[j] = result[:, :, j * wc : (j + 1) * wc]
    for d in range(1, F):
        remote(fs_buf.at[ahead(d)], fr_buf.at[me_f], f_ssem.at[d], f_rsem.at[d], me_r, ahead(d)).start()
    fr_buf[me_f] = fs_buf[me_f]
    for d in range(1, F):
        remote(fs_buf.at[ahead(d)], fr_buf.at[behind(d)], f_ssem.at[d], f_rsem.at[d], me_r, ahead(d)).wait()
    for f in range(F):
        out_ref[:, :, :, f * oc : (f + 1) * oc] = fr_buf[f].astype(BF16)


def solution(mesh):
    F, R = mesh.shape["frame"], mesh.shape["row"]

    def local(
        latent, qkv_weight, out_weight, attn_gain, in_weight, depth_weight, down_weight, mlp_gain, conv_first,
        conv_second,
    ):
        fl, h, W, C = latent.shape
        T = fl * F
        hc = qkv_weight.shape[1]
        N = in_weight.shape[2]
        oc = conv_first.shape[3]
        sums = -(-T // 16) * 16
        vmem = pl.BlockSpec(memory_space=pltpu.VMEM)
        hbm = pl.BlockSpec(memory_space=pl.ANY)
        dma = lambda count: pltpu.SemaphoreType.DMA((count,))
        return pl.pallas_call(
            functools.partial(kernel, F, R),
            out_shape=jax.ShapeDtypeStruct((T, h, W // F, C), BF16),
            in_specs=[vmem, vmem, vmem, vmem, hbm, vmem, hbm, vmem, hbm, hbm],
            out_specs=vmem,
            scratch_shapes=[
                pltpu.VMEM((T, h + 2, W, C), BF16),
                pltpu.VMEM((F, hc, C), BF16),
                pltpu.VMEM((R, T * HEAD + sums, hc), BF16),
                pltpu.VMEM((F, T * (h + 2) * W, hc), BF16),
                pltpu.VMEM((T, h + 2, W, C), BF16),
                pltpu.VMEM((T, h, W, C), F32),
                pltpu.VMEM((T, h, W, C), BF16),
                pltpu.VMEM((F, fl, h, W, C), BF16),
                pltpu.VMEM((fl, h, W, C), BF16),
                pltpu.VMEM((T, h + 4, W, C), BF16),
                pltpu.VMEM((3, T + 2, h + 4, W, C), BF16),
                pltpu.VMEM((F, T * (h + 2) * W, oc), BF16),
                pltpu.VMEM((3, T + 2, h + 2, W, C), BF16),
                pltpu.VMEM((F, T, h, W // F, oc), F32),
                pltpu.VMEM((F, T, h, W // F, oc), F32),
                pltpu.VMEM((2, C, N), BF16),
                pltpu.VMEM(down_weight.shape, BF16),
                pltpu.VMEM(conv_first.shape, BF16),
                pltpu.VMEM(conv_second.shape, BF16),
                dma(4),
                dma(3 * F), dma(3 * F),
                dma(F), dma(F),
                dma(R), dma(R),
                dma(F), dma(F),
                dma(F), dma(F),
                dma(3 * F), dma(3 * F),
                dma(F), dma(F),
                dma(F), dma(F),
            ],
            compiler_params=pltpu.CompilerParams(collective_id=0, has_side_effects=True),
        )(
            latent, qkv_weight, out_weight, attn_gain.reshape(1, C), jnp.transpose(in_weight, (1, 0, 2)),
            depth_weight, down_weight, mlp_gain.reshape(1, C), conv_first, conv_second,
        )

    in_specs = (
        P(("parts", "frame"), "row", None, None),
        P(None, "frame", None),
        P("frame", None),
        P(),
        P(None, None, "frame"),
        P(),
        P("frame", None),
        P(),
        P(None, None, None, "frame", None),
        P(None, None, None, "frame", None),
    )
    out_specs = P("parts", "row", "frame", None)
    return jax.shard_map(local, mesh=mesh, in_specs=in_specs, out_specs=out_specs, check_vma=False)
```

```python
import functools

import jax
import jax.numpy as jnp
from jax import lax
from jax.experimental import pallas as pl
from jax.experimental.pallas import tpu as pltpu
from jax.sharding import PartitionSpec as P

HEAD = 32
F32 = jnp.float32
BF16 = jnp.bfloat16
MESH = pl.DeviceIdType.MESH


def dot(a, b):
    return jnp.dot(a, b, preferred_element_type=F32)


def dot_nt(a, b):
    return lax.dot_general(a, b, (((1,), (1,)), ((), ())), preferred_element_type=F32)


def dot_tn(a, b):
    return lax.dot_general(a, b, (((0,), (0,)), ((), ())), preferred_element_type=F32)


def split(values):
    high = values.astype(BF16)
    return high, (values - high.astype(F32)).astype(BF16)


def norm_rows(values, gain):
    return values * lax.rsqrt(jnp.mean(values * values, axis=-1, keepdims=True) + 1e-05) * gain


def column_shifts(flat, columns):
    count = flat.shape[0]
    at = lax.rem(lax.broadcasted_iota(jnp.int32, flat.shape, 0), columns)
    left = jnp.where(at == 0, 0.0, pltpu.roll(flat, 1, 0))
    right = jnp.where(at == columns - 1, 0.0, pltpu.roll(flat, count - 1, 0))
    return left, flat, right


def kernel(
    F,
    R,
    latent_ref,
    qkv_ref,
    out_w_ref,
    attn_gain_ref,
    in_w_hbm,
    depth_ref,
    down_hbm,
    mlp_gain_ref,
    first_hbm,
    second_hbm,
    out_ref,
    x_buf,
    ow_buf,
    st_buf,
    mx_buf,
    fi_buf,
    part_buf,
    rs_send,
    rs_buf,
    own_buf,
    s_buf,
    sh_buf,
    h_buf,
    hs_buf,
    fs_buf,
    fr_buf,
    in_raw,
    in_w,
    down_w,
    first_w,
    second_w,
    load_sem,
    x_ssem,
    x_rsem,
    ow_ssem,
    ow_rsem,
    st_ssem,
    st_rsem,
    mx_ssem,
    mx_rsem,
    rs_ssem,
    rs_rsem,
    s_ssem,
    s_rsem,
    h_ssem,
    h_rsem,
    f_ssem,
    f_rsem,
):
    me_f = lax.axis_index("frame")
    me_r = lax.axis_index("row")
    fl, h, W, C = latent_ref.shape
    T = fl * F
    hc = qkv_ref.shape[1]
    N = in_w.shape[2]
    oc = first_w.shape[3]
    heads = hc // HEAD
    wc = W // F

    loads = [
        pltpu.make_async_copy(src, dst, load_sem.at[i])
        for i, (src, dst) in enumerate(
            ((in_w_hbm, in_raw), (down_hbm, down_w), (first_hbm, first_w), (second_hbm, second_w))
        )
    ]
    for load in loads:
        load.start()

    chip, core, chips = lax.div(me_f, 2), lax.rem(me_f, 2), F // 2

    def chip_behind(e):
        return lax.rem(chip + (chips - e), chips)

    def ahead(d):
        return 2 * lax.rem(chip + d // 2, chips) + lax.rem(core + d, 2)

    def behind(d):
        return 2 * chip_behind(d // 2) + lax.rem(core + d, 2)

    def remote(src, dst, ssem, rsem, row, frame):
        return pltpu.make_async_remote_copy(
            src_ref=src,
            dst_ref=dst,
            send_sem=ssem,
            recv_sem=rsem,
            device_id={"row": row, "frame": frame},
            device_id_type=MESH,
        )

    barrier = pltpu.get_barrier_semaphore()

    def greet(row, frame):
        pl.semaphore_signal(barrier, inc=1, device_id={"row": row, "frame": frame}, device_id_type=MESH)

    for d in range(1, F):
        greet(me_r, ahead(d))
    for d in range(1, R):
        greet(lax.rem(me_r + d, R), me_f)

    @pl.when(me_r < R - 1)
    def _():
        for d in range(1, F):
            greet(me_r + 1, ahead(d))

    @pl.when(me_r > 0)
    def _():
        for d in range(1, F):
            greet(me_r - 1, ahead(d))

    neighbours = lax.div(me_r + (R - 1), R) + lax.div(2 * R - 2 - me_r, R)
    pl.semaphore_wait(barrier, F - 1 + R - 1 + (F - 1) * neighbours)

    def frames_of(index):
        return pl.ds(index * fl, fl)

    def band_start(src, buf, g, ssem, rsem):
        mine = frames_of(me_f)
        for d in reversed(range(1, F)):
            remote(src, buf.at[mine, g : g + h], ssem.at[d], rsem.at[d], me_r, ahead(d)).start()

        @pl.when(me_r < R - 1)
        def _():
            for d in reversed(range(F)):
                remote(
                    src.at[:, h - g : h], buf.at[mine, 0:g], ssem.at[F + d], rsem.at[F + d], me_r + 1, ahead(d)
                ).start()

        @pl.when(me_r > 0)
        def _():
            for d in reversed(range(F)):
                remote(
                    src.at[:, 0:g], buf.at[mine, g + h : h + 2 * g], ssem.at[2 * F + d], rsem.at[2 * F + d],
                    me_r - 1, ahead(d),
                ).start()

    def band_wait_own(src, buf, g, ssem, rsem, d):
        remote(src, buf.at[frames_of(behind(d)), g : g + h], ssem.at[d], rsem.at[d], me_r, ahead(d)).wait()

    def band_wait_edges(src, buf, g, ssem, rsem):
        @pl.when(me_r > 0)
        def _():
            for d in range(F):
                theirs = frames_of(behind(d))
                remote(
                    src.at[:, 0:g], buf.at[theirs, 0:g], ssem.at[2 * F + d], rsem.at[F + d], me_r - 1, ahead(d)
                ).wait()

        @pl.when(me_r < R - 1)
        def _():
            for d in range(F):
                theirs = frames_of(behind(d))
                remote(
                    src.at[:, h - g : h], buf.at[theirs, g + h : h + 2 * g], ssem.at[F + d], rsem.at[2 * F + d],
                    me_r + 1, ahead(d),
                ).wait()

    def zero_edges(buf, g):
        @pl.when(me_r == 0)
        def _():
            buf[:, 0:g] = jnp.zeros((T, g, W, C), BF16)

        @pl.when(me_r == R - 1)
        def _():
            buf[:, g + h : h + 2 * g] = jnp.zeros((T, g, W, C), BF16)

    def share_start(buf, ssem, rsem, src=None):
        for d in reversed(range(1, F)):
            remote(
                buf.at[me_f] if src is None else src, buf.at[me_f], ssem.at[d], rsem.at[d], me_r, ahead(d)
            ).start()

    def share_wait(buf, ssem, rsem, src=None, peers=range(1, F)):
        for d in peers:
            remote(
                buf.at[me_f] if src is None else src, buf.at[behind(d)], ssem.at[d], rsem.at[d], me_r, ahead(d)
            ).wait()

    band_start(latent_ref, x_buf, 1, x_ssem, x_rsem)
    x_buf[frames_of(me_f), 1 : 1 + h] = latent_ref[...]
    zero_edges(x_buf, 1)
    zero_edges(s_buf, 2)
    ow_buf[me_f] = out_w_ref[...]
    for shift in range(3):
        for t in (0, T + 1):
            sh_buf[shift, t] = jnp.zeros(sh_buf.shape[2:], BF16)
            hs_buf[:, shift, t] = jnp.zeros((chips, *hs_buf.shape[3:]), BF16)
    for d in range(1, F):
        band_wait_own(latent_ref, x_buf, 1, x_ssem, x_rsem, d)

    own_x = x_buf[:, 1 : 1 + h].reshape(T * h * W, C)
    keys = jnp.maximum(dot_nt(own_x, qkv_ref[1]), 0.0).astype(BF16)
    values = dot_nt(own_x, qkv_ref[2]).astype(BF16)
    head_row = lax.div(lax.broadcasted_iota(jnp.int32, (hc, hc), 0), HEAD)
    head_col = lax.div(lax.broadcasted_iota(jnp.int32, (hc, hc), 1), HEAD)
    same_head = head_row == head_col
    n = h * W
    for t in range(T):
        outer = dot_tn(keys[t * n : (t + 1) * n], values[t * n : (t + 1) * n])
        outer = jnp.where(same_head, outer, 0.0)
        packed = outer[0:HEAD]
        for i in range(1, heads):
            packed = packed + outer[i * HEAD : (i + 1) * HEAD]
        st_buf[me_r, t * HEAD : (t + 1) * HEAD] = packed.astype(BF16)
    sums = st_buf.shape[1] - T * HEAD
    of_frame = lax.div(lax.broadcasted_iota(jnp.int32, (sums, T * n), 1), n)
    pick = jnp.where(of_frame == lax.broadcasted_iota(jnp.int32, (sums, T * n), 0), 1.0, 0.0).astype(BF16)
    st_buf[me_r, T * HEAD :] = dot(pick, keys).astype(BF16)
    for d in range(1, R):
        remote(
            st_buf.at[me_r], st_buf.at[me_r], st_ssem.at[d], st_rsem.at[d], lax.rem(me_r + d, R), me_f
        ).start()
    share_start(ow_buf, ow_ssem, ow_rsem, out_w_ref)
    band_wait_edges(latent_ref, x_buf, 1, x_ssem, x_rsem)
    query = jnp.maximum(dot_nt(x_buf[...].reshape(T * (h + 2) * W, C), qkv_ref[0]), 0.0).astype(BF16)
    loads[0].wait()
    for k in range(2):
        in_w[k] = in_raw[:, k, :]
    for d in range(1, R):
        remote(
            st_buf.at[me_r], st_buf.at[lax.rem(me_r + (R - d), R)], st_ssem.at[d], st_rsem.at[d],
            lax.rem(me_r + d, R), me_f,
        ).wait()
    total = st_buf[0].astype(F32)
    for r in range(1, R):
        total = total + st_buf[r].astype(F32)
    total = total * (1.0 / (h * R * W))

    ones = jnp.where(same_head, 1.0, 0.0).astype(BF16)
    m = (h + 2) * W
    for t in range(T):
        q = query[t * m : (t + 1) * m]
        packed = total[t * HEAD : (t + 1) * HEAD]
        state = jnp.where(same_head, jnp.concatenate([packed] * heads, axis=0), 0.0)
        high, low = split(state)
        numer = dot(q, high) + dot(q, low)
        high, low = split(q.astype(F32) * total[T * HEAD + t : T * HEAD + t + 1])
        denom = jnp.maximum(dot(high, ones) + dot(low, ones), 1.0)
        mx_buf[me_f, t * m : (t + 1) * m] = (numer / denom).astype(BF16)
    share_start(mx_buf, mx_ssem, mx_rsem)
    share_wait(ow_buf, ow_ssem, ow_rsem, out_w_ref)
    share_wait(mx_buf, mx_ssem, mx_rsem)

    attn_out = dot(mx_buf[0], ow_buf[0])
    for f in range(1, F):
        attn_out = attn_out + dot(mx_buf[f], ow_buf[f])
    latent = x_buf[...].reshape(T * m, C).astype(F32)
    first = (latent + norm_rows(attn_out, attn_gain_ref[...])).astype(BF16)
    fi_buf[...] = first.reshape(T, h + 2, W, C)

    spread = []
    lanes = pl.ds(pl.multiple_of(me_f * N, N), N)
    for k in range(2):
        inner = jax.nn.silu(dot(first, in_w[k])).astype(BF16).astype(F32)
        mix = jnp.zeros((T, h, W, N), F32)
        for j, moved in enumerate(column_shifts(inner, W)):
            moved = moved.reshape(T, h + 2, W, N)
            for i in range(3):
                tap = depth_ref[i, j, k : k + 1, lanes]
                mix = mix + moved[:, i : i + h] * tap.reshape(1, 1, 1, N)
        spread.append(mix)
    gated = (spread[0] * jax.nn.silu(spread[1])).astype(BF16).reshape(T * n, N)
    loads[1].wait()
    part = dot(gated, down_w[...]).reshape(T, h, W, C)
    part_buf[...] = part
    rs_send[...] = part.astype(BF16)
    for d in range(1, F):
        remote(
            rs_send.at[frames_of(ahead(d))], rs_buf.at[d], rs_ssem.at[d], rs_rsem.at[d], me_r, ahead(d)
        ).start()
    for d in range(1, F):
        remote(
            rs_send.at[frames_of(ahead(d))], rs_buf.at[d], rs_ssem.at[d], rs_rsem.at[d], me_r, ahead(d)
        ).wait()
    mlp_out = part_buf[frames_of(me_f)]
    for d in range(1, F):
        mlp_out = mlp_out + rs_buf[d].astype(F32)
    second = (
        fi_buf[frames_of(me_f), 1 : 1 + h].astype(F32)
        + norm_rows(mlp_out, mlp_gain_ref[...].reshape(1, 1, 1, C))
    ).astype(BF16)
    own_buf[...] = second
    band_start(own_buf, s_buf, 2, s_ssem, s_rsem)
    s_buf[frames_of(me_f), 2 : 2 + h] = second

    def place(frames, at, count, start, rows):
        flat = s_buf[frames, start : start + rows].reshape(count * rows * W, C).astype(F32)
        for j, moved in enumerate(column_shifts(flat, W)):
            sh_buf[j, at, start : start + rows] = moved.astype(BF16).reshape(count, rows, W, C)

    def place_own(f):
        place(frames_of(f), pl.ds(1 + f * fl, fl), fl, 2, h)

    place_own(me_f)
    for d in range(1, F):
        band_wait_own(own_buf, s_buf, 2, s_ssem, s_rsem, d)
        place_own(behind(d))
    band_wait_edges(own_buf, s_buf, 2, s_ssem, s_rsem)
    for start in (0, h + 2):
        place(slice(0, T), slice(1, T + 1), T, start, 2)
    loads[2].wait()

    def conv(acc, buf, weight, out_rows):
        for a in range(3):
            for b in range(3):
                for c in range(3):
                    slab = buf[c, a : a + T, b : b + out_rows].reshape(T * out_rows * W, buf.shape[-1])
                    acc = acc + dot_nt(slab, weight(a, b, c))
        return acc

    active = jax.nn.silu(
        conv(jnp.zeros((T * (h + 2) * W, oc), F32), sh_buf, lambda a, b, c: first_w[a, b, c], h + 2)
    )
    row = lax.rem(lax.div(lax.broadcasted_iota(jnp.int32, active.shape, 0), W), h + 2) + (me_r * h - 1)
    hidden = jnp.where((row >= 0) & (row < h * R), active, 0.0)
    h_buf[me_f] = hidden.astype(BF16)
    share_start(h_buf, h_ssem, h_rsem)
    loads[3].wait()

    result = jnp.zeros((T * n, oc), F32)
    for e in range(chips):
        share_wait(h_buf, h_ssem, h_rsem, peers=range(max(2 * e, 1), 2 * e + 2))
        source = chip_behind(e)
        for i in range(2):
            for j, moved in enumerate(column_shifts(h_buf[2 * source + i].astype(F32), W)):
                hs_buf[e, j, 1 : T + 1, :, :, i * oc : (i + 1) * oc] = moved.astype(BF16).reshape(T, h + 2, W, oc)
        taken = pl.ds(pl.multiple_of(source * 2 * oc, 2 * oc), 2 * oc)
        result = conv(result, hs_buf.at[e], lambda a, b, c: second_w[a, b, c, :, taken], h)
    for f in range(F):
        kept = s_buf[:, 2 : 2 + h, :, f * oc : (f + 1) * oc].astype(F32).reshape(T * n, oc)
        result = result + jnp.where(me_f == f, kept, 0.0)
    result = result.reshape(T, h, W, oc)
    for j in range(F):
        fs_buf[j] = result[:, :, j * wc : (j + 1) * wc].astype(BF16)
    for d in range(1, F):
        remote(fs_buf.at[ahead(d)], fr_buf.at[me_f], f_ssem.at[d], f_rsem.at[d], me_r, ahead(d)).start()
    fr_buf[me_f] = fs_buf[me_f]
    for d in range(1, F):
        remote(fs_buf.at[ahead(d)], fr_buf.at[behind(d)], f_ssem.at[d], f_rsem.at[d], me_r, ahead(d)).wait()
    for f in range(F):
        out_ref[:, :, :, f * oc : (f + 1) * oc] = fr_buf[f]


def solution(mesh):
    F, R = mesh.shape["frame"], mesh.shape["row"]

    def local(
        latent, qkv_weight, out_weight, attn_gain, in_weight, depth_weight, down_weight, mlp_gain, conv_first,
        conv_second,
    ):
        fl, h, W, C = latent.shape
        T = fl * F
        hc = qkv_weight.shape[1]
        N = in_weight.shape[2]
        oc = conv_first.shape[3]
        sums = -(-T // 16) * 16
        vmem = pl.BlockSpec(memory_space=pltpu.VMEM)
        hbm = pl.BlockSpec(memory_space=pl.ANY)
        dma = lambda count: pltpu.SemaphoreType.DMA((count,))
        return pl.pallas_call(
            functools.partial(kernel, F, R),
            out_shape=jax.ShapeDtypeStruct((T, h, W // F, C), BF16),
            in_specs=[vmem, vmem, vmem, vmem, hbm, vmem, hbm, vmem, hbm, hbm],
            out_specs=vmem,
            scratch_shapes=[
                pltpu.VMEM((T, h + 2, W, C), BF16),
                pltpu.VMEM((F, hc, C), BF16),
                pltpu.VMEM((R, T * HEAD + sums, hc), BF16),
                pltpu.VMEM((F, T * (h + 2) * W, hc), BF16),
                pltpu.VMEM((T, h + 2, W, C), BF16),
                pltpu.VMEM((T, h, W, C), F32),
                pltpu.VMEM((T, h, W, C), BF16),
                pltpu.VMEM((F, fl, h, W, C), BF16),
                pltpu.VMEM((fl, h, W, C), BF16),
                pltpu.VMEM((T, h + 4, W, C), BF16),
                pltpu.VMEM((3, T + 2, h + 4, W, C), BF16),
                pltpu.VMEM((F, T * (h + 2) * W, oc), BF16),
                pltpu.VMEM((F // 2, 3, T + 2, h + 2, W, 2 * oc), BF16),
                pltpu.VMEM((F, T, h, W // F, oc), BF16),
                pltpu.VMEM((F, T, h, W // F, oc), BF16),
                pltpu.VMEM((C, 2, N), BF16),
                pltpu.VMEM((2, C, N), BF16),
                pltpu.VMEM(down_weight.shape, BF16),
                pltpu.VMEM(conv_first.shape, BF16),
                pltpu.VMEM(conv_second.shape, BF16),
                dma(4),
                dma(3 * F), dma(3 * F),
                dma(F), dma(F),
                dma(R), dma(R),
                dma(F), dma(F),
                dma(F), dma(F),
                dma(3 * F), dma(3 * F),
                dma(F), dma(F),
                dma(F), dma(F),
            ],
            compiler_params=pltpu.CompilerParams(collective_id=0, has_side_effects=True),
        )(
            latent, qkv_weight, out_weight, attn_gain.reshape(1, C), in_weight,
            depth_weight, down_weight, mlp_gain.reshape(1, C), conv_first, conv_second,
        )

    in_specs = (
        P(("parts", "frame"), "row", None, None),
        P(None, "frame", None),
        P("frame", None),
        P(),
        P(None, None, "frame"),
        P(),
        P("frame", None),
        P(),
        P(None, None, None, "frame", None),
        P(None, None, None, "frame", None),
    )
    out_specs = P("parts", "row", "frame", None)
    return jax.shard_map(local, mesh=mesh, in_specs=in_specs, out_specs=out_specs, check_vma=False)
```

```python
import functools

import jax
import jax.numpy as jnp
from jax import lax
from jax.experimental import pallas as pl
from jax.experimental.pallas import tpu as pltpu
from jax.sharding import PartitionSpec as P

HEAD = 32
F32 = jnp.float32
BF16 = jnp.bfloat16
MESH = pl.DeviceIdType.MESH


def dot(a, b):
    return jnp.dot(a, b, preferred_element_type=F32)


def dot_nt(a, b):
    return lax.dot_general(a, b, (((1,), (1,)), ((), ())), preferred_element_type=F32)


def dot_tn(a, b):
    return lax.dot_general(a, b, (((0,), (0,)), ((), ())), preferred_element_type=F32)


def split(values):
    high = values.astype(BF16)
    return high, (values - high.astype(F32)).astype(BF16)


def norm_rows(values, gain):
    return values * lax.rsqrt(jnp.mean(values * values, axis=-1, keepdims=True) + 1e-05) * gain


def column_shifts(flat, columns):
    count = flat.shape[0]
    at = lax.rem(lax.broadcasted_iota(jnp.int32, flat.shape, 0), columns)
    left = jnp.where(at == 0, 0.0, pltpu.roll(flat, 1, 0))
    right = jnp.where(at == columns - 1, 0.0, pltpu.roll(flat, count - 1, 0))
    return left, flat, right


def kernel(
    F,
    R,
    latent_ref,
    qkv_hbm,
    out_w_ref,
    attn_gain_hbm,
    in_w_hbm,
    depth_hbm,
    down_hbm,
    mlp_gain_hbm,
    first_hbm,
    second_hbm,
    out_ref,
    x_buf,
    ow_buf,
    st_buf,
    mx_buf,
    fi_buf,
    part_buf,
    rs_send,
    rs_buf,
    own_buf,
    s_buf,
    sh_buf,
    h_buf,
    hs_buf,
    fs_buf,
    fr_buf,
    qkv_ref,
    depth_ref,
    attn_gain_ref,
    mlp_gain_ref,
    in_raw,
    in_w,
    down_w,
    first_w,
    second_w,
    load_sem,
    x_ssem,
    x_rsem,
    ow_ssem,
    ow_rsem,
    st_ssem,
    st_rsem,
    mx_ssem,
    mx_rsem,
    rs_ssem,
    rs_rsem,
    s_ssem,
    s_rsem,
    h_ssem,
    h_rsem,
    f_ssem,
    f_rsem,
):
    me_f = lax.axis_index("frame")
    me_r = lax.axis_index("row")
    fl, h, W, C = latent_ref.shape
    T = fl * F
    hc = qkv_ref.shape[1]
    N = in_w.shape[2]
    oc = first_w.shape[3]
    heads = hc // HEAD
    wc = W // F

    chip, core, chips = lax.div(me_f, 2), lax.rem(me_f, 2), F // 2

    def chip_behind(e):
        return lax.rem(chip + (chips - e), chips)

    def ahead(d):
        return 2 * lax.rem(chip + d // 2, chips) + lax.rem(core + d, 2)

    def behind(d):
        return 2 * chip_behind(d // 2) + lax.rem(core + d, 2)

    def remote(src, dst, ssem, rsem, row, frame):
        return pltpu.make_async_remote_copy(
            src_ref=src,
            dst_ref=dst,
            send_sem=ssem,
            recv_sem=rsem,
            device_id={"row": row, "frame": frame},
            device_id_type=MESH,
        )

    pairs = (
        (in_w_hbm, in_raw),
        (down_hbm, down_w),
        (first_hbm, first_w),
        (second_hbm, second_w),
        (latent_ref, x_buf.at[pl.ds(me_f * fl, fl), 1 : 1 + h]),
        (qkv_hbm, qkv_ref),
        (out_w_ref, ow_buf.at[me_f]),
        (attn_gain_hbm, attn_gain_ref),
        (depth_hbm, depth_ref),
        (mlp_gain_hbm, mlp_gain_ref),
    )
    loads = [pltpu.make_async_copy(src, dst, load_sem.at[i]) for i, (src, dst) in enumerate(pairs)]
    loads[4].start()
    loads[5].start()

    barrier = pltpu.get_barrier_semaphore()

    def greet(row, frame):
        pl.semaphore_signal(barrier, inc=1, device_id={"row": row, "frame": frame}, device_id_type=MESH)

    for d in range(1, F):
        greet(me_r, ahead(d))
    for d in range(1, R):
        greet(lax.rem(me_r + d, R), me_f)

    @pl.when(me_r < R - 1)
    def _():
        for d in range(1, F):
            greet(me_r + 1, ahead(d))

    @pl.when(me_r > 0)
    def _():
        for d in range(1, F):
            greet(me_r - 1, ahead(d))

    neighbours = lax.div(me_r + (R - 1), R) + lax.div(2 * R - 2 - me_r, R)
    pl.semaphore_wait(barrier, F - 1 + R - 1 + (F - 1) * neighbours)

    def frames_of(index):
        return pl.ds(index * fl, fl)

    def band_start(src, buf, g, ssem, rsem):
        mine = frames_of(me_f)
        for d in reversed(range(1, F)):
            remote(src, buf.at[mine, g : g + h], ssem.at[d], rsem.at[d], me_r, ahead(d)).start()

        @pl.when(me_r < R - 1)
        def _():
            for d in reversed(range(F)):
                remote(
                    src.at[:, h - g : h], buf.at[mine, 0:g], ssem.at[F + d], rsem.at[F + d], me_r + 1, ahead(d)
                ).start()

        @pl.when(me_r > 0)
        def _():
            for d in reversed(range(F)):
                remote(
                    src.at[:, 0:g], buf.at[mine, g + h : h + 2 * g], ssem.at[2 * F + d], rsem.at[2 * F + d],
                    me_r - 1, ahead(d),
                ).start()

    def band_wait_own(src, buf, g, ssem, rsem, d):
        remote(src, buf.at[frames_of(behind(d)), g : g + h], ssem.at[d], rsem.at[d], me_r, ahead(d)).wait()

    def band_wait_edges(src, buf, g, ssem, rsem):
        @pl.when(me_r > 0)
        def _():
            for d in range(F):
                theirs = frames_of(behind(d))
                remote(
                    src.at[:, 0:g], buf.at[theirs, 0:g], ssem.at[2 * F + d], rsem.at[F + d], me_r - 1, ahead(d)
                ).wait()

        @pl.when(me_r < R - 1)
        def _():
            for d in range(F):
                theirs = frames_of(behind(d))
                remote(
                    src.at[:, h - g : h], buf.at[theirs, g + h : h + 2 * g], ssem.at[F + d], rsem.at[2 * F + d],
                    me_r + 1, ahead(d),
                ).wait()

    def zero_edges(buf, g):
        @pl.when(me_r == 0)
        def _():
            buf[:, 0:g] = jnp.zeros((T, g, W, C), BF16)

        @pl.when(me_r == R - 1)
        def _():
            buf[:, g + h : h + 2 * g] = jnp.zeros((T, g, W, C), BF16)

    def share_start(buf, ssem, rsem, src=None):
        for d in reversed(range(1, F)):
            remote(
                buf.at[me_f] if src is None else src, buf.at[me_f], ssem.at[d], rsem.at[d], me_r, ahead(d)
            ).start()

    def share_wait(buf, ssem, rsem, src=None, peers=range(1, F)):
        for d in peers:
            remote(
                buf.at[me_f] if src is None else src, buf.at[behind(d)], ssem.at[d], rsem.at[d], me_r, ahead(d)
            ).wait()

    band_start(latent_ref, x_buf, 1, x_ssem, x_rsem)
    for i in (6, 0, 7, 8, 9, 1, 2, 3):
        loads[i].start()
    zero_edges(x_buf, 1)
    zero_edges(s_buf, 2)
    for shift in range(3):
        for t in (0, T + 1):
            sh_buf[shift, t] = jnp.zeros(sh_buf.shape[2:], BF16)
            hs_buf[:, shift, t] = jnp.zeros((chips, *hs_buf.shape[3:]), BF16)
    for d in range(1, F):
        band_wait_own(latent_ref, x_buf, 1, x_ssem, x_rsem, d)
    loads[4].wait()
    loads[5].wait()

    own_x = x_buf[:, 1 : 1 + h].reshape(T * h * W, C)
    keys = jnp.maximum(dot_nt(own_x, qkv_ref[1]), 0.0).astype(BF16)
    values = dot_nt(own_x, qkv_ref[2]).astype(BF16)
    head_row = lax.div(lax.broadcasted_iota(jnp.int32, (hc, hc), 0), HEAD)
    head_col = lax.div(lax.broadcasted_iota(jnp.int32, (hc, hc), 1), HEAD)
    same_head = head_row == head_col
    n = h * W
    for t in range(T):
        outer = dot_tn(keys[t * n : (t + 1) * n], values[t * n : (t + 1) * n])
        outer = jnp.where(same_head, outer, 0.0)
        packed = outer[0:HEAD]
        for i in range(1, heads):
            packed = packed + outer[i * HEAD : (i + 1) * HEAD]
        st_buf[me_r, t * HEAD : (t + 1) * HEAD] = packed.astype(BF16)
    sums = st_buf.shape[1] - T * HEAD
    of_frame = lax.div(lax.broadcasted_iota(jnp.int32, (sums, T * n), 1), n)
    pick = jnp.where(of_frame == lax.broadcasted_iota(jnp.int32, (sums, T * n), 0), 1.0, 0.0).astype(BF16)
    st_buf[me_r, T * HEAD :] = dot(pick, keys).astype(BF16)
    for d in range(1, R):
        remote(
            st_buf.at[me_r], st_buf.at[me_r], st_ssem.at[d], st_rsem.at[d], lax.rem(me_r + d, R), me_f
        ).start()
    share_start(ow_buf, ow_ssem, ow_rsem, out_w_ref)
    band_wait_edges(latent_ref, x_buf, 1, x_ssem, x_rsem)
    query = jnp.maximum(dot_nt(x_buf[...].reshape(T * (h + 2) * W, C), qkv_ref[0]), 0.0).astype(BF16)
    loads[0].wait()
    for k in range(2):
        in_w[k] = in_raw[:, k, :]
    for d in range(1, R):
        remote(
            st_buf.at[me_r], st_buf.at[lax.rem(me_r + (R - d), R)], st_ssem.at[d], st_rsem.at[d],
            lax.rem(me_r + d, R), me_f,
        ).wait()
    total = st_buf[0].astype(F32)
    for r in range(1, R):
        total = total + st_buf[r].astype(F32)
    total = total * (1.0 / (h * R * W))

    ones = jnp.where(same_head, 1.0, 0.0).astype(BF16)
    m = (h + 2) * W
    for t in range(T):
        q = query[t * m : (t + 1) * m]
        packed = total[t * HEAD : (t + 1) * HEAD]
        state = jnp.where(same_head, jnp.concatenate([packed] * heads, axis=0), 0.0)
        high, low = split(state)
        numer = dot(q, high) + dot(q, low)
        high, low = split(q.astype(F32) * total[T * HEAD + t : T * HEAD + t + 1])
        denom = jnp.maximum(dot(high, ones) + dot(low, ones), 1.0)
        mx_buf[me_f, t * m : (t + 1) * m] = (numer / denom).astype(BF16)
    share_start(mx_buf, mx_ssem, mx_rsem)
    share_wait(ow_buf, ow_ssem, ow_rsem, out_w_ref)
    share_wait(mx_buf, mx_ssem, mx_rsem)

    for i in (6, 7, 8, 9, 1):
        loads[i].wait()

    lanes = pl.ds(pl.multiple_of(me_f * N, N), N)
    for e in [*range(1, chips), 0]:
        target = lax.rem(chip + e, chips)
        count = 2 * fl
        taken = pl.ds(target * count, count)
        tokens = pl.ds(pl.multiple_of(target * (count * m), count * m), count * m)
        attn_out = dot(mx_buf[0, tokens], ow_buf[0])
        for f in range(1, F):
            attn_out = attn_out + dot(mx_buf[f, tokens], ow_buf[f])
        latent = x_buf[taken].reshape(count * m, C).astype(F32)
        first = (latent + norm_rows(attn_out, attn_gain_ref[...])).astype(BF16)
        if e == 0:
            fi_buf[taken] = first.reshape(count, h + 2, W, C)

        spread = []
        for k in range(2):
            inner = jax.nn.silu(dot(first, in_w[k])).astype(BF16).astype(F32)
            mix = jnp.zeros((count, h, W, N), F32)
            for j, moved in enumerate(column_shifts(inner, W)):
                moved = moved.reshape(count, h + 2, W, N)
                for i in range(3):
                    tap = depth_ref[i, j, k : k + 1, lanes]
                    mix = mix + moved[:, i : i + h] * tap.reshape(1, 1, 1, N)
            spread.append(mix)
        gated = (spread[0] * jax.nn.silu(spread[1])).astype(BF16).reshape(count * n, N)
        part = dot(gated, down_w[...]).reshape(count, h, W, C)
        if e == 0:
            part_buf[taken] = part
        rs_send[taken] = part.astype(BF16)
        for d in range(max(2 * e, 1), 2 * e + 2):
            remote(
                rs_send.at[frames_of(ahead(d))], rs_buf.at[d], rs_ssem.at[d], rs_rsem.at[d], me_r, ahead(d)
            ).start()
    for d in range(1, F):
        remote(
            rs_send.at[frames_of(ahead(d))], rs_buf.at[d], rs_ssem.at[d], rs_rsem.at[d], me_r, ahead(d)
        ).wait()
    mlp_out = part_buf[frames_of(me_f)]
    for d in range(1, F):
        mlp_out = mlp_out + rs_buf[d].astype(F32)
    second = (
        fi_buf[frames_of(me_f), 1 : 1 + h].astype(F32)
        + norm_rows(mlp_out, mlp_gain_ref[...].reshape(1, 1, 1, C))
    ).astype(BF16)
    own_buf[...] = second
    band_start(own_buf, s_buf, 2, s_ssem, s_rsem)
    s_buf[frames_of(me_f), 2 : 2 + h] = second

    def place(frames, at, count, start, rows):
        flat = s_buf[frames, start : start + rows].reshape(count * rows * W, C).astype(F32)
        for j, moved in enumerate(column_shifts(flat, W)):
            sh_buf[j, at, start : start + rows] = moved.astype(BF16).reshape(count, rows, W, C)

    def place_own(f):
        place(frames_of(f), pl.ds(1 + f * fl, fl), fl, 2, h)

    place_own(me_f)
    for d in range(1, F):
        band_wait_own(own_buf, s_buf, 2, s_ssem, s_rsem, d)
        place_own(behind(d))
    band_wait_edges(own_buf, s_buf, 2, s_ssem, s_rsem)
    for start in (0, h + 2):
        place(slice(0, T), slice(1, T + 1), T, start, 2)
    loads[2].wait()

    def conv(acc, buf, weight, out_rows):
        for a in range(3):
            for b in range(3):
                for c in range(3):
                    slab = buf[c, a : a + T, b : b + out_rows].reshape(T * out_rows * W, buf.shape[-1])
                    acc = acc + dot_nt(slab, weight(a, b, c))
        return acc

    active = jax.nn.silu(
        conv(jnp.zeros((T * (h + 2) * W, oc), F32), sh_buf, lambda a, b, c: first_w[a, b, c], h + 2)
    )
    row = lax.rem(lax.div(lax.broadcasted_iota(jnp.int32, active.shape, 0), W), h + 2) + (me_r * h - 1)
    hidden = jnp.where((row >= 0) & (row < h * R), active, 0.0)
    h_buf[me_f] = hidden.astype(BF16)
    share_start(h_buf, h_ssem, h_rsem)
    loads[3].wait()

    result = jnp.zeros((T * n, oc), F32)
    for e in range(chips):
        share_wait(h_buf, h_ssem, h_rsem, peers=range(max(2 * e, 1), 2 * e + 2))
        source = chip_behind(e)
        for i in range(2):
            for j, moved in enumerate(column_shifts(h_buf[2 * source + i].astype(F32), W)):
                hs_buf[e, j, 1 : T + 1, :, :, i * oc : (i + 1) * oc] = moved.astype(BF16).reshape(T, h + 2, W, oc)
        taken = pl.ds(pl.multiple_of(source * 2 * oc, 2 * oc), 2 * oc)
        result = conv(result, hs_buf.at[e], lambda a, b, c: second_w[a, b, c, :, taken], h)
    for f in range(F):
        kept = s_buf[:, 2 : 2 + h, :, f * oc : (f + 1) * oc].astype(F32).reshape(T * n, oc)
        result = result + jnp.where(me_f == f, kept, 0.0)
    result = result.reshape(T, h, W, oc)
    for j in range(F):
        fs_buf[j] = result[:, :, j * wc : (j + 1) * wc].astype(BF16)
    for d in range(1, F):
        remote(fs_buf.at[ahead(d)], fr_buf.at[me_f], f_ssem.at[d], f_rsem.at[d], me_r, ahead(d)).start()
    fr_buf[me_f] = fs_buf[me_f]
    for d in range(1, F):
        remote(fs_buf.at[ahead(d)], fr_buf.at[behind(d)], f_ssem.at[d], f_rsem.at[d], me_r, ahead(d)).wait()
    for f in range(F):
        out_ref[:, :, :, f * oc : (f + 1) * oc] = fr_buf[f]


def solution(mesh):
    F, R = mesh.shape["frame"], mesh.shape["row"]

    def local(
        latent, qkv_weight, out_weight, attn_gain, in_weight, depth_weight, down_weight, mlp_gain, conv_first,
        conv_second,
    ):
        fl, h, W, C = latent.shape
        T = fl * F
        hc = qkv_weight.shape[1]
        N = in_weight.shape[2]
        oc = conv_first.shape[3]
        sums = -(-T // 16) * 16
        vmem = pl.BlockSpec(memory_space=pltpu.VMEM)
        hbm = pl.BlockSpec(memory_space=pl.ANY)
        dma = lambda count: pltpu.SemaphoreType.DMA((count,))
        return pl.pallas_call(
            functools.partial(kernel, F, R),
            out_shape=jax.ShapeDtypeStruct((T, h, W // F, C), BF16),
            in_specs=[hbm] * 10,
            out_specs=vmem,
            scratch_shapes=[
                pltpu.VMEM((T, h + 2, W, C), BF16),
                pltpu.VMEM((F, hc, C), BF16),
                pltpu.VMEM((R, T * HEAD + sums, hc), BF16),
                pltpu.VMEM((F, T * (h + 2) * W, hc), BF16),
                pltpu.VMEM((T, h + 2, W, C), BF16),
                pltpu.VMEM((T, h, W, C), F32),
                pltpu.VMEM((T, h, W, C), BF16),
                pltpu.VMEM((F, fl, h, W, C), BF16),
                pltpu.VMEM((fl, h, W, C), BF16),
                pltpu.VMEM((T, h + 4, W, C), BF16),
                pltpu.VMEM((3, T + 2, h + 4, W, C), BF16),
                pltpu.VMEM((F, T * (h + 2) * W, oc), BF16),
                pltpu.VMEM((F // 2, 3, T + 2, h + 2, W, 2 * oc), BF16),
                pltpu.VMEM((F, T, h, W // F, oc), BF16),
                pltpu.VMEM((F, T, h, W // F, oc), BF16),
                pltpu.VMEM(qkv_weight.shape, BF16),
                pltpu.VMEM(depth_weight.shape, F32),
                pltpu.VMEM((1, C), F32),
                pltpu.VMEM((1, C), F32),
                pltpu.VMEM((C, 2, N), BF16),
                pltpu.VMEM((2, C, N), BF16),
                pltpu.VMEM(down_weight.shape, BF16),
                pltpu.VMEM(conv_first.shape, BF16),
                pltpu.VMEM(conv_second.shape, BF16),
                dma(10),
                dma(3 * F), dma(3 * F),
                dma(F), dma(F),
                dma(R), dma(R),
                dma(F), dma(F),
                dma(F), dma(F),
                dma(3 * F), dma(3 * F),
                dma(F), dma(F),
                dma(F), dma(F),
            ],
            compiler_params=pltpu.CompilerParams(collective_id=0, has_side_effects=True),
        )(
            latent, qkv_weight, out_weight, attn_gain.reshape(1, C), in_weight,
            depth_weight, down_weight, mlp_gain.reshape(1, C), conv_first, conv_second,
        )

    in_specs = (
        P(("parts", "frame"), "row", None, None),
        P(None, "frame", None),
        P("frame", None),
        P(),
        P(None, None, "frame"),
        P(),
        P("frame", None),
        P(),
        P(None, None, None, "frame", None),
        P(None, None, None, "frame", None),
    )
    out_specs = P("parts", "row", "frame", None)
    return jax.shard_map(local, mesh=mesh, in_specs=in_specs, out_specs=out_specs, check_vma=False)
```

```python
import functools

import jax
import jax.numpy as jnp
from jax import lax
from jax.experimental import pallas as pl
from jax.experimental.pallas import tpu as pltpu
from jax.sharding import PartitionSpec as P

HEAD = 32
F32 = jnp.float32
BF16 = jnp.bfloat16
MESH = pl.DeviceIdType.MESH


def dot(a, b):
    return jnp.dot(a, b, preferred_element_type=F32)


def dot_nt(a, b):
    return lax.dot_general(a, b, (((1,), (1,)), ((), ())), preferred_element_type=F32)


def dot_tn(a, b):
    return lax.dot_general(a, b, (((0,), (0,)), ((), ())), preferred_element_type=F32)


def split(values):
    high = values.astype(BF16)
    return high, (values - high.astype(F32)).astype(BF16)


def norm_rows(values, gain):
    return values * lax.rsqrt(jnp.mean(values * values, axis=-1, keepdims=True) + 1e-05) * gain


def column_shifts(flat, columns):
    count = flat.shape[0]
    at = lax.rem(lax.broadcasted_iota(jnp.int32, flat.shape, 0), columns)
    left = jnp.where(at == 0, 0.0, pltpu.roll(flat, 1, 0))
    right = jnp.where(at == columns - 1, 0.0, pltpu.roll(flat, count - 1, 0))
    return left, flat, right


def kernel(
    F,
    R,
    latent_ref,
    qkv_hbm,
    out_w_ref,
    attn_gain_hbm,
    in_w_hbm,
    depth_hbm,
    down_hbm,
    mlp_gain_hbm,
    first_hbm,
    second_hbm,
    out_ref,
    x_buf,
    ow_buf,
    st_buf,
    mx_buf,
    fi_buf,
    part_buf,
    rs_send,
    rs_buf,
    own_buf,
    s_buf,
    sh_buf,
    h_buf,
    hs_buf,
    fs_buf,
    fr_buf,
    qkv_ref,
    depth_ref,
    attn_gain_ref,
    mlp_gain_ref,
    in_raw,
    in_w,
    down_w,
    first_w,
    second_w,
    load_sem,
    x_ssem,
    x_rsem,
    ow_ssem,
    ow_rsem,
    st_ssem,
    st_rsem,
    mx_ssem,
    mx_rsem,
    rs_ssem,
    rs_rsem,
    s_ssem,
    s_rsem,
    h_ssem,
    h_rsem,
    f_ssem,
    f_rsem,
):
    me_f = lax.axis_index("frame")
    me_r = lax.axis_index("row")
    fl, h, W, C = latent_ref.shape
    T = fl * F
    hc = qkv_ref.shape[1]
    N = in_w.shape[2]
    oc = first_w.shape[3]
    heads = hc // HEAD
    wc = W // F

    chip, core, chips = lax.div(me_f, 2), lax.rem(me_f, 2), F // 2

    def chip_behind(e):
        return lax.rem(chip + (chips - e), chips)

    def ahead(d):
        return 2 * lax.rem(chip + d // 2, chips) + lax.rem(core + d, 2)

    def behind(d):
        return 2 * chip_behind(d // 2) + lax.rem(core + d, 2)

    def remote(src, dst, ssem, rsem, row, frame):
        return pltpu.make_async_remote_copy(
            src_ref=src,
            dst_ref=dst,
            send_sem=ssem,
            recv_sem=rsem,
            device_id={"row": row, "frame": frame},
            device_id_type=MESH,
        )

    pairs = (
        (in_w_hbm, in_raw),
        (down_hbm, down_w),
        (first_hbm, first_w),
        (second_hbm, second_w),
        (latent_ref, x_buf.at[pl.ds(me_f * fl, fl), 1 : 1 + h]),
        (qkv_hbm, qkv_ref),
        (out_w_ref, ow_buf.at[me_f]),
        (attn_gain_hbm, attn_gain_ref),
        (depth_hbm, depth_ref),
        (mlp_gain_hbm, mlp_gain_ref),
    )
    loads = [pltpu.make_async_copy(src, dst, load_sem.at[i]) for i, (src, dst) in enumerate(pairs)]
    loads[4].start()
    loads[5].start()

    barrier = pltpu.get_barrier_semaphore()

    def greet(row, frame):
        pl.semaphore_signal(barrier, inc=1, device_id={"row": row, "frame": frame}, device_id_type=MESH)

    for d in range(1, F):
        greet(me_r, ahead(d))
    for d in range(1, R):
        greet(lax.rem(me_r + d, R), me_f)

    @pl.when(me_r < R - 1)
    def _():
        for d in range(1, F):
            greet(me_r + 1, ahead(d))

    @pl.when(me_r > 0)
    def _():
        for d in range(1, F):
            greet(me_r - 1, ahead(d))

    neighbours = lax.div(me_r + (R - 1), R) + lax.div(2 * R - 2 - me_r, R)
    pl.semaphore_wait(barrier, F - 1 + R - 1 + (F - 1) * neighbours)

    def frames_of(index):
        return pl.ds(index * fl, fl)

    def band_start(src, buf, g, ssem, rsem):
        mine = frames_of(me_f)
        for d in reversed(range(1, F)):
            remote(src, buf.at[mine, g : g + h], ssem.at[d], rsem.at[d], me_r, ahead(d)).start()

        @pl.when(me_r < R - 1)
        def _():
            for d in reversed(range(F)):
                remote(
                    src.at[:, h - g : h], buf.at[mine, 0:g], ssem.at[F + d], rsem.at[F + d], me_r + 1, ahead(d)
                ).start()

        @pl.when(me_r > 0)
        def _():
            for d in reversed(range(F)):
                remote(
                    src.at[:, 0:g], buf.at[mine, g + h : h + 2 * g], ssem.at[2 * F + d], rsem.at[2 * F + d],
                    me_r - 1, ahead(d),
                ).start()

    def band_wait_own(src, buf, g, ssem, rsem, d):
        remote(src, buf.at[frames_of(behind(d)), g : g + h], ssem.at[d], rsem.at[d], me_r, ahead(d)).wait()

    def band_wait_edges(src, buf, g, ssem, rsem):
        @pl.when(me_r > 0)
        def _():
            for d in range(F):
                theirs = frames_of(behind(d))
                remote(
                    src.at[:, 0:g], buf.at[theirs, 0:g], ssem.at[2 * F + d], rsem.at[F + d], me_r - 1, ahead(d)
                ).wait()

        @pl.when(me_r < R - 1)
        def _():
            for d in range(F):
                theirs = frames_of(behind(d))
                remote(
                    src.at[:, h - g : h], buf.at[theirs, g + h : h + 2 * g], ssem.at[F + d], rsem.at[2 * F + d],
                    me_r + 1, ahead(d),
                ).wait()

    def zero_edges(buf, g):
        @pl.when(me_r == 0)
        def _():
            buf[:, 0:g] = jnp.zeros((T, g, W, C), BF16)

        @pl.when(me_r == R - 1)
        def _():
            buf[:, g + h : h + 2 * g] = jnp.zeros((T, g, W, C), BF16)

    def share_start(buf, ssem, rsem, src=None):
        for d in reversed(range(1, F)):
            remote(
                buf.at[me_f] if src is None else src, buf.at[me_f], ssem.at[d], rsem.at[d], me_r, ahead(d)
            ).start()

    def share_wait(buf, ssem, rsem, src=None, peers=range(1, F)):
        for d in peers:
            remote(
                buf.at[me_f] if src is None else src, buf.at[behind(d)], ssem.at[d], rsem.at[d], me_r, ahead(d)
            ).wait()

    band_start(latent_ref, x_buf, 1, x_ssem, x_rsem)
    for i in (6, 0, 7, 8, 9, 1, 2, 3):
        loads[i].start()
    zero_edges(x_buf, 1)
    zero_edges(s_buf, 2)
    for t in (0, T + 1):
        sh_buf[t] = jnp.zeros(sh_buf.shape[1:], BF16)
        hs_buf[:, t] = jnp.zeros((chips, *hs_buf.shape[2:]), BF16)
    for d in range(1, F):
        band_wait_own(latent_ref, x_buf, 1, x_ssem, x_rsem, d)
    loads[4].wait()
    loads[5].wait()

    own_x = x_buf[:, 1 : 1 + h].reshape(T * h * W, C)
    keys = jnp.maximum(dot_nt(own_x, qkv_ref[1]), 0.0).astype(BF16)
    values = dot_nt(own_x, qkv_ref[2]).astype(BF16)
    head_row = lax.div(lax.broadcasted_iota(jnp.int32, (hc, hc), 0), HEAD)
    head_col = lax.div(lax.broadcasted_iota(jnp.int32, (hc, hc), 1), HEAD)
    same_head = head_row == head_col
    n = h * W
    for t in range(T):
        outer = dot_tn(keys[t * n : (t + 1) * n], values[t * n : (t + 1) * n])
        outer = jnp.where(same_head, outer, 0.0)
        packed = outer[0:HEAD]
        for i in range(1, heads):
            packed = packed + outer[i * HEAD : (i + 1) * HEAD]
        st_buf[me_r, t * HEAD : (t + 1) * HEAD] = packed.astype(BF16)
    sums = st_buf.shape[1] - T * HEAD
    of_frame = lax.div(lax.broadcasted_iota(jnp.int32, (sums, T * n), 1), n)
    pick = jnp.where(of_frame == lax.broadcasted_iota(jnp.int32, (sums, T * n), 0), 1.0, 0.0).astype(BF16)
    st_buf[me_r, T * HEAD :] = dot(pick, keys).astype(BF16)
    for d in range(1, R):
        remote(
            st_buf.at[me_r], st_buf.at[me_r], st_ssem.at[d], st_rsem.at[d], lax.rem(me_r + d, R), me_f
        ).start()
    share_start(ow_buf, ow_ssem, ow_rsem, out_w_ref)
    band_wait_edges(latent_ref, x_buf, 1, x_ssem, x_rsem)
    query = jnp.maximum(dot_nt(x_buf[...].reshape(T * (h + 2) * W, C), qkv_ref[0]), 0.0).astype(BF16)
    loads[0].wait()
    for k in range(2):
        in_w[k] = in_raw[:, k, :]
    for d in range(1, R):
        remote(
            st_buf.at[me_r], st_buf.at[lax.rem(me_r + (R - d), R)], st_ssem.at[d], st_rsem.at[d],
            lax.rem(me_r + d, R), me_f,
        ).wait()
    total = st_buf[0].astype(F32)
    for r in range(1, R):
        total = total + st_buf[r].astype(F32)
    total = total * (1.0 / (h * R * W))

    ones = jnp.where(same_head, 1.0, 0.0).astype(BF16)
    m = (h + 2) * W
    for t in range(T):
        q = query[t * m : (t + 1) * m]
        packed = total[t * HEAD : (t + 1) * HEAD]
        state = jnp.where(same_head, jnp.concatenate([packed] * heads, axis=0), 0.0)
        high, low = split(state)
        numer = dot(q, high) + dot(q, low)
        high, low = split(q.astype(F32) * total[T * HEAD + t : T * HEAD + t + 1])
        denom = jnp.maximum(dot(high, ones) + dot(low, ones), 1.0)
        mx_buf[me_f, t * m : (t + 1) * m] = (numer / denom).astype(BF16)
    share_start(mx_buf, mx_ssem, mx_rsem)
    share_wait(ow_buf, ow_ssem, ow_rsem, out_w_ref)
    share_wait(mx_buf, mx_ssem, mx_rsem)

    for i in (6, 7, 8, 9, 1):
        loads[i].wait()

    lanes = pl.ds(pl.multiple_of(me_f * N, N), N)
    for e in [*range(1, chips), 0]:
        target = lax.rem(chip + e, chips)
        count = 2 * fl
        taken = pl.ds(target * count, count)
        tokens = pl.ds(pl.multiple_of(target * (count * m), count * m), count * m)
        attn_out = dot(mx_buf[0, tokens], ow_buf[0])
        for f in range(1, F):
            attn_out = attn_out + dot(mx_buf[f, tokens], ow_buf[f])
        latent = x_buf[taken].reshape(count * m, C).astype(F32)
        first = (latent + norm_rows(attn_out, attn_gain_ref[...])).astype(BF16)
        if e == 0:
            fi_buf[taken] = first.reshape(count, h + 2, W, C)

        spread = []
        for k in range(2):
            inner = jax.nn.silu(dot(first, in_w[k])).astype(BF16).astype(F32)
            mix = jnp.zeros((count, h, W, N), F32)
            for j, moved in enumerate(column_shifts(inner, W)):
                moved = moved.reshape(count, h + 2, W, N)
                for i in range(3):
                    tap = depth_ref[i, j, k : k + 1, lanes]
                    mix = mix + moved[:, i : i + h] * tap.reshape(1, 1, 1, N)
            spread.append(mix)
        gated = (spread[0] * jax.nn.silu(spread[1])).astype(BF16).reshape(count * n, N)
        part = dot(gated, down_w[...]).reshape(count, h, W, C)
        if e == 0:
            part_buf[taken] = part
        rs_send[taken] = part.astype(BF16)
        for d in range(max(2 * e, 1), 2 * e + 2):
            remote(
                rs_send.at[frames_of(ahead(d))], rs_buf.at[d], rs_ssem.at[d], rs_rsem.at[d], me_r, ahead(d)
            ).start()
    for d in range(1, F):
        remote(
            rs_send.at[frames_of(ahead(d))], rs_buf.at[d], rs_ssem.at[d], rs_rsem.at[d], me_r, ahead(d)
        ).wait()
    mlp_out = part_buf[frames_of(me_f)]
    for d in range(1, F):
        mlp_out = mlp_out + rs_buf[d].astype(F32)
    second = (
        fi_buf[frames_of(me_f), 1 : 1 + h].astype(F32)
        + norm_rows(mlp_out, mlp_gain_ref[...].reshape(1, 1, 1, C))
    ).astype(BF16)
    own_buf[...] = second
    band_start(own_buf, s_buf, 2, s_ssem, s_rsem)
    s_buf[frames_of(me_f), 2 : 2 + h] = second

    def place(frames, at, start, rows):
        sh_buf[at, start : start + rows] = s_buf[frames, start : start + rows]

    def place_own(f):
        place(frames_of(f), pl.ds(1 + f * fl, fl), 2, h)

    place_own(me_f)
    for d in range(1, F):
        band_wait_own(own_buf, s_buf, 2, s_ssem, s_rsem, d)
        place_own(behind(d))
    band_wait_edges(own_buf, s_buf, 2, s_ssem, s_rsem)
    for start in (0, h + 2):
        place(slice(0, T), slice(1, T + 1), start, 2)
    loads[2].wait()

    def conv(acc, buf, weight, out_rows):
        for a in range(3):
            for b in range(3):
                slab = buf[a : a + T, b : b + out_rows].reshape(T * out_rows * W, buf.shape[-1])
                acc = acc + dot_nt(slab, weight(a, b))
        return acc

    def join(acc):
        return (
            column_shifts(acc[:, 0:oc], W)[0]
            + acc[:, oc : 2 * oc]
            + column_shifts(acc[:, 2 * oc : 3 * oc], W)[2]
        )

    taps = conv(
        jnp.zeros((T * (h + 2) * W, 3 * oc), F32), sh_buf, lambda a, b: first_w[a, b].reshape(3 * oc, C), h + 2
    )
    active = jax.nn.silu(join(taps))
    row = lax.rem(lax.div(lax.broadcasted_iota(jnp.int32, active.shape, 0), W), h + 2) + (me_r * h - 1)
    hidden = jnp.where((row >= 0) & (row < h * R), active, 0.0)
    h_buf[me_f] = hidden.astype(BF16)
    share_start(h_buf, h_ssem, h_rsem)
    loads[3].wait()

    taps = jnp.zeros((T * n, 3 * oc), F32)
    for e in range(chips):
        share_wait(h_buf, h_ssem, h_rsem, peers=range(max(2 * e, 1), 2 * e + 2))
        source = chip_behind(e)
        for i in range(2):
            hs_buf[e, 1 : T + 1, :, :, i * oc : (i + 1) * oc] = h_buf[2 * source + i].reshape(T, h + 2, W, oc)
        taken = pl.ds(pl.multiple_of(source * 2 * oc, 2 * oc), 2 * oc)
        taps = conv(
            taps, hs_buf.at[e], lambda a, b: second_w[a, b, :, :, taken].reshape(3 * oc, 2 * oc), h
        )
    result = join(taps)
    for f in range(F):
        kept = s_buf[:, 2 : 2 + h, :, f * oc : (f + 1) * oc].astype(F32).reshape(T * n, oc)
        result = result + jnp.where(me_f == f, kept, 0.0)
    result = result.reshape(T, h, W, oc)
    for j in range(F):
        fs_buf[j] = result[:, :, j * wc : (j + 1) * wc].astype(BF16)
    for d in range(1, F):
        remote(fs_buf.at[ahead(d)], fr_buf.at[me_f], f_ssem.at[d], f_rsem.at[d], me_r, ahead(d)).start()
    fr_buf[me_f] = fs_buf[me_f]
    for d in range(1, F):
        remote(fs_buf.at[ahead(d)], fr_buf.at[behind(d)], f_ssem.at[d], f_rsem.at[d], me_r, ahead(d)).wait()
    for f in range(F):
        out_ref[:, :, :, f * oc : (f + 1) * oc] = fr_buf[f]


def solution(mesh):
    F, R = mesh.shape["frame"], mesh.shape["row"]

    def local(
        latent, qkv_weight, out_weight, attn_gain, in_weight, depth_weight, down_weight, mlp_gain, conv_first,
        conv_second,
    ):
        fl, h, W, C = latent.shape
        T = fl * F
        hc = qkv_weight.shape[1]
        N = in_weight.shape[2]
        oc = conv_first.shape[3]
        sums = -(-T // 16) * 16
        vmem = pl.BlockSpec(memory_space=pltpu.VMEM)
        hbm = pl.BlockSpec(memory_space=pl.ANY)
        dma = lambda count: pltpu.SemaphoreType.DMA((count,))
        return pl.pallas_call(
            functools.partial(kernel, F, R),
            out_shape=jax.ShapeDtypeStruct((T, h, W // F, C), BF16),
            in_specs=[hbm] * 10,
            out_specs=vmem,
            scratch_shapes=[
                pltpu.VMEM((T, h + 2, W, C), BF16),
                pltpu.VMEM((F, hc, C), BF16),
                pltpu.VMEM((R, T * HEAD + sums, hc), BF16),
                pltpu.VMEM((F, T * (h + 2) * W, hc), BF16),
                pltpu.VMEM((T, h + 2, W, C), BF16),
                pltpu.VMEM((T, h, W, C), F32),
                pltpu.VMEM((T, h, W, C), BF16),
                pltpu.VMEM((F, fl, h, W, C), BF16),
                pltpu.VMEM((fl, h, W, C), BF16),
                pltpu.VMEM((T, h + 4, W, C), BF16),
                pltpu.VMEM((T + 2, h + 4, W, C), BF16),
                pltpu.VMEM((F, T * (h + 2) * W, oc), BF16),
                pltpu.VMEM((F // 2, T + 2, h + 2, W, 2 * oc), BF16),
                pltpu.VMEM((F, T, h, W // F, oc), BF16),
                pltpu.VMEM((F, T, h, W // F, oc), BF16),
                pltpu.VMEM(qkv_weight.shape, BF16),
                pltpu.VMEM(depth_weight.shape, F32),
                pltpu.VMEM((1, C), F32),
                pltpu.VMEM((1, C), F32),
                pltpu.VMEM((C, 2, N), BF16),
                pltpu.VMEM((2, C, N), BF16),
                pltpu.VMEM(down_weight.shape, BF16),
                pltpu.VMEM(conv_first.shape, BF16),
                pltpu.VMEM(conv_second.shape, BF16),
                dma(10),
                dma(3 * F), dma(3 * F),
                dma(F), dma(F),
                dma(R), dma(R),
                dma(F), dma(F),
                dma(F), dma(F),
                dma(3 * F), dma(3 * F),
                dma(F), dma(F),
                dma(F), dma(F),
            ],
            compiler_params=pltpu.CompilerParams(collective_id=0, has_side_effects=True),
        )(
            latent, qkv_weight, out_weight, attn_gain.reshape(1, C), in_weight,
            depth_weight, down_weight, mlp_gain.reshape(1, C), conv_first, conv_second,
        )

    in_specs = (
        P(("parts", "frame"), "row", None, None),
        P(None, "frame", None),
        P("frame", None),
        P(),
        P(None, None, "frame"),
        P(),
        P("frame", None),
        P(),
        P(None, None, None, "frame", None),
        P(None, None, None, "frame", None),
    )
    out_specs = P("parts", "row", "frame", None)
    return jax.shard_map(local, mesh=mesh, in_specs=in_specs, out_specs=out_specs, check_vma=False)
```
